32 devices in a mesh: dp: 8 (over z, core), tensor: 4 (over y, x).
Axes of the slice: x: 2, y: 2, z: 4, core: 2. Of those that a mesh axis runs over, the one named last changes fastest.
Arguments:
- token_ids: int32 [4096], P('dp'), may hold values from 0 to 511
- seq_lengths: int32 [16], P('dp'), may hold values from 32 to 256
- embed_table: bfloat16 [512, 8192], P('dp', 'tensor'), may hold values from -420 to 420
- norm_gain: float32 [8192], replicated, may hold values from 0.1 to 1.9
- query_weight: bfloat16 [8192, 8192], P('tensor', 'dp'), may hold values from -1.3479223 to 1.3479223
- kv_weight: bfloat16 [2048, 8192], P('tensor', 'dp'), may hold values from -0.044194174 to 0.044194174
Outputs:
- attention_out: bfloat16 [4096, 8192], P('dp', 'tensor')
The draws below stay inside these ranges and needn't reach their ends.
All inputs are finite; a program needn't handle non-finite values.
Results may differ from the reference program's by a relative error of at most 0.0091.
Values may be sent and summed in bfloat16 or wider, within the bound.
A program may use at most 128 MiB of HBM per device.

```python
import math
import jax
import jax.numpy as jnp
import numpy as np
from jax import lax

D = 8192
HD = 128
HEADS = 64
KV_HEADS = 8
VOCAB = 512
SEQ = 256
TOKENS = 4096
SEQS = 16


def weights_common(key):
    folded = jax.random.fold_in(key, 101)
    key_keys, key_values, key_noise = jax.random.split(folded, 3)
    key_matrix = jax.random.truncated_normal(key_keys, -4.0, 4.0, (KV_HEADS, HD, D), jnp.float32) * D ** (-0.5)
    value_matrix = jax.random.truncated_normal(key_values, -4.0, 4.0, (KV_HEADS, HD, D), jnp.float32) * D ** (-0.5)
    query_noise = jax.random.truncated_normal(key_noise, -4.0, 4.0, (HEADS, HD, D), jnp.float32) * D ** (-0.5)
    return (key_matrix, value_matrix, query_noise)


def draw_query_weight(key, part):
    key_matrix, value_matrix, query_noise = weights_common(key)
    weights = query_noise
    return weights.reshape(HEADS * HD, D).astype(jnp.bfloat16)


def draw_kv_weight(key, part):
    key_matrix, value_matrix, query_noise = weights_common(key)
    stacked = jnp.stack((key_matrix, value_matrix), axis=0)
    return stacked.reshape(2 * KV_HEADS * HD, D).astype(jnp.bfloat16)


def draw_embed_table(key, part):
    folded = jax.random.fold_in(key, 202)
    key_rows, key_columns, key_entries = jax.random.split(folded, 3)
    column_scale = 3.0 ** (jnp.arange(D, dtype=jnp.float32) / D)[None, :]
    column_scale = column_scale * jnp.exp(jax.random.uniform(key_columns, (1, D), jnp.float32, 0.0, math.log(3.4)))
    row_scale = jnp.exp(jax.random.uniform(key_rows, (VOCAB, 1), jnp.float32, 0.0, math.log(10.0)))
    entries = jax.random.truncated_normal(key_entries, -4.0, 4.0, (VOCAB, D), jnp.float32)
    return (entries * row_scale * column_scale).astype(jnp.bfloat16)


def with_ends(values, own_key, low, top_value):
    extent = values.shape
    spot = [jax.random.randint(jax.random.fold_in(own_key, axis), (), 0, extent[axis]) for axis in range(len(extent))]
    values = values.at[tuple(spot)].set(low)
    longest = extent.index(max(extent))
    spot[longest] = (spot[longest] + 1) % extent[longest]
    return values.at[tuple(spot)].set(top_value)


def rank_table(amount, skew):
    weights = [(1 << 20) // math.isqrt(grade ** skew) + 1 for grade in range(1, amount + 1)]
    scale = 1 + sum(weights) // (1 << 30)
    return np.cumsum(np.array([max(1, weight // scale) for weight in weights]))


def ranked(own_key, shape, amount, lean):
    table = rank_table(amount, lean)
    pick = jax.random.randint(jax.random.fold_in(own_key, 1), shape, 0, int(table[amount - 1]))
    grade = jnp.searchsorted(jnp.asarray(table, jnp.int32), pick, side="right")
    return jax.random.permutation(jax.random.fold_in(own_key, 2), amount)[grade].astype(jnp.int32)


def setup_inputs(seed: int = 0) -> dict:
    key_list = jax.random.split(jax.random.key(seed), 7)
    token_ids = with_ends(ranked(key_list[0], (TOKENS,), VOCAB, 2), jax.random.fold_in(key_list[0], 3), 0, VOCAB - 1).astype(jnp.int32)
    seq_lengths = with_ends(jax.random.randint(key_list[1], (SEQS,), max(1, SEQ // 8), SEQ + 1), jax.random.fold_in(key_list[1], 1), max(1, SEQ // 8), SEQ).astype(jnp.int32)
    embed_table = draw_embed_table(jax.random.fold_in(key_list[6], 71), 0)
    norm_gain = jnp.clip(1.0 + 0.18 * jax.random.normal(key_list[3], (D,), jnp.float32), 0.1, 1.9)
    query_weight = draw_query_weight(jax.random.fold_in(key_list[6], 71), 0)
    kv_weight = draw_kv_weight(jax.random.fold_in(key_list[6], 71), 0)
    return dict(token_ids=token_ids, seq_lengths=seq_lengths, embed_table=embed_table, norm_gain=norm_gain, query_weight=query_weight, kv_weight=kv_weight)


epsilon = 1e-05
rope_base = 500000.0

def rope_tables(positions, head_size):
    halfway = head_size // 2
    frequencies = rope_base ** (-(jnp.arange(halfway, dtype=jnp.float32) * 2.0 / head_size))
    angles = positions.astype(jnp.float32)[:, None] * frequencies[None, :]
    return (jnp.cos(angles), jnp.sin(angles))

def rotate_last(values, cosine, sine_vals):
    halfway = values.shape[-1] // 2
    lower = values[..., :halfway]
    upper = values[..., halfway:]
    return jnp.concatenate([lower * cosine - upper * sine_vals, upper * cosine + lower * sine_vals], axis=-1)

def reference(token_ids, seq_lengths, embed_table, norm_gain, query_weight, kv_weight):
    embedded = embed_table.astype(jnp.float32)[token_ids]
    mean_square = lax.optimization_barrier(jnp.mean(embedded * embedded, axis=1, keepdims=True))
    normed = (embedded * lax.rsqrt(mean_square + epsilon) * norm_gain[None, :]).astype(jnp.bfloat16)
    queries = jnp.dot(normed, query_weight.T, preferred_element_type=jnp.float32)
    keyvals = jnp.dot(normed, kv_weight.T, preferred_element_type=jnp.float32).astype(jnp.bfloat16)
    positions = jnp.arange(TOKENS, dtype=jnp.int32) % SEQ
    cosine, sine_vals = rope_tables(positions, HD)
    cosine = cosine[:, None, :]
    sine_vals = sine_vals[:, None, :]
    rot_queries = rotate_last(queries.reshape(TOKENS, HEADS, HD), cosine, sine_vals).astype(jnp.bfloat16)
    kv_split = keyvals.reshape(TOKENS, 2, KV_HEADS, HD)
    rot_keys = rotate_last(kv_split[:, 0].astype(jnp.float32), cosine, sine_vals).astype(jnp.bfloat16)
    values_all = kv_split[:, 1]
    group_size = HEADS // KV_HEADS

    def attend_one(inputs):
        query_seq, key_seq, value_seq, length = inputs
        key_rep = jnp.repeat(key_seq, group_size, axis=1).astype(jnp.float32)
        value_rep = jnp.repeat(value_seq, group_size, axis=1).astype(jnp.float32)
        scores = jnp.einsum('qhd,khd->hqk', query_seq.astype(jnp.float32), key_rep) / math.sqrt(HD)
        slots = jnp.arange(SEQ, dtype=jnp.int32)
        allowed = (slots[None, :] <= slots[:, None]) & (slots[None, :] < length)
        scores = jnp.where(allowed[None], scores, -1e+30)
        largest = lax.optimization_barrier(jnp.max(scores, axis=-1, keepdims=True))
        exponent = jnp.exp(scores - largest)
        probs = (exponent / lax.optimization_barrier(jnp.sum(exponent, axis=-1, keepdims=True))).astype(jnp.bfloat16)
        attended = jnp.einsum('hqk,khd->qhd', probs.astype(jnp.float32), value_rep)
        return attended.astype(jnp.bfloat16).reshape(SEQ, HEADS * HD)
    per_sequence = lax.map(attend_one, (rot_queries.reshape(SEQS, SEQ, HEADS, HD), rot_keys.reshape(SEQS, SEQ, KV_HEADS, HD), values_all.reshape(SEQS, SEQ, KV_HEADS, HD), seq_lengths))
    return per_sequence.reshape(TOKENS, HEADS * HD)
```

```python
import math

import jax
import jax.numpy as jnp
from jax import lax
from jax.sharding import PartitionSpec as P

HD = 128
HEADS = 64
KV_HEADS = 8
SEQ = 256


epsilon = 1e-05
rope_base = 500000.0


def rope_tables(positions, head_size):
    halfway = head_size // 2
    frequencies = rope_base ** (-(jnp.arange(halfway, dtype=jnp.float32) * 2.0 / head_size))
    angles = positions.astype(jnp.float32)[:, None] * frequencies[None, :]
    return (jnp.cos(angles), jnp.sin(angles))


def rotate_last(values, cosine, sine_vals):
    halfway = values.shape[-1] // 2
    lower = values[..., :halfway]
    upper = values[..., halfway:]
    return jnp.concatenate(
        [lower * cosine - upper * sine_vals, upper * cosine + lower * sine_vals], axis=-1
    )


def on_device(token_ids, seq_lengths, embed_table, norm_gain, query_weight, kv_weight):
    tok_rows = token_ids.shape[0]
    tensor_index = lax.axis_index("tensor")
    tensor_count = lax.axis_size("tensor")
    heads_here = query_weight.shape[0] // HD
    group_size = HEADS // KV_HEADS
    kv_count = max(1, heads_here // group_size)
    per_group = heads_here // kv_count
    first_kv = tensor_index * heads_here // group_size
    rows = lax.all_gather(embed_table, "tensor", axis=1, tiled=True).astype(jnp.float32)
    mean_square = jnp.mean(rows * rows, axis=1, keepdims=True)
    normed_rows = (rows * lax.rsqrt(mean_square + epsilon) * norm_gain[None, :]).astype(jnp.bfloat16)
    normed = lax.all_to_all(normed_rows, "dp", split_axis=1, concat_axis=0, tiled=True)
    vocab_size = normed.shape[0]
    kv_grid = lax.all_gather(kv_weight, "tensor", axis=0, tiled=True).reshape(2, KV_HEADS, HD, -1)
    kv_rows = lax.dynamic_slice_in_dim(kv_grid, first_kv, kv_count, 1).reshape(2 * kv_count * HD, -1)
    weights = jnp.concatenate([query_weight, kv_rows], axis=0)
    partial = lax.dot_general(
        normed, weights, (((1,), (1,)), ((), ())), preferred_element_type=jnp.float32
    )
    summed = lax.psum_scatter(partial, "dp", scatter_dimension=0, tiled=True)
    table = lax.all_gather(summed.astype(jnp.bfloat16), "dp", axis=0, tiled=True)
    one_hot = (token_ids[:, None] == jnp.arange(vocab_size, dtype=jnp.int32)[None, :]).astype(
        jnp.bfloat16
    )
    picked = jnp.dot(one_hot, table, preferred_element_type=jnp.float32)
    q_width = heads_here * HD
    queries = picked[:, :q_width]
    seq_count = tok_rows // SEQ
    positions = jnp.arange(tok_rows, dtype=jnp.int32) % SEQ
    cosine, sine_vals = rope_tables(positions, HD)
    rot_queries = rotate_last(
        queries.reshape(tok_rows, heads_here, HD), cosine[:, None, :], sine_vals[:, None, :]
    ).astype(jnp.bfloat16)
    local = picked[:, q_width:].reshape(tok_rows, 2, kv_count, HD)
    rot_keys = rotate_last(
        local[:, 0], cosine[:, None, :], sine_vals[:, None, :]
    ).astype(jnp.bfloat16)
    query_grid = rot_queries.reshape(seq_count, SEQ, kv_count, per_group, HD)
    key_grid = rot_keys.reshape(seq_count, SEQ, kv_count, HD)
    value_grid = local[:, 1].astype(jnp.bfloat16).reshape(seq_count, SEQ, kv_count, HD)
    scores = jnp.einsum(
        "sqghd,skgd->sghqk", query_grid, key_grid, preferred_element_type=jnp.float32
    ) / math.sqrt(HD)
    slots = jnp.arange(SEQ, dtype=jnp.int32)
    causal = slots[None, :] <= slots[:, None]
    live = slots[None, :] < seq_lengths[:, None]
    allowed = causal[None, :, :] & live[:, None, :]
    scores = jnp.where(allowed[:, None, None, :, :], scores, -1e30)
    largest = jnp.max(scores, axis=-1, keepdims=True)
    exponent = jnp.exp(scores - largest)
    probs = (exponent / jnp.sum(exponent, axis=-1, keepdims=True)).astype(jnp.bfloat16)
    attended = jnp.einsum(
        "sghqk,skgd->sqghd", probs, value_grid, preferred_element_type=jnp.float32
    )
    return attended.astype(jnp.bfloat16).reshape(tok_rows, heads_here * HD)


def solution(mesh):
    placed = (P("dp"), P("dp"), P("dp", "tensor"), P(), P("tensor", "dp"), P("tensor", "dp"))
    return jax.shard_map(
        on_device, mesh=mesh, in_specs=placed, out_specs=P("dp", "tensor"), check_vma=False
    )
```

```python
import math

import functools

import jax
import jax.numpy as jnp
import numpy as np
from jax import lax
from jax.experimental import pallas as pl
from jax.experimental.pallas import tpu as pltpu
from jax.sharding import PartitionSpec as P

HD = 128
HEADS = 64
KV_HEADS = 8
SEQ = 256


epsilon = 1e-05
rope_base = 500000.0


MESH = pl.DeviceIdType.MESH
F32 = jnp.float32
BF16 = jnp.bfloat16
WIDE = 256


def rope_tables():
    halfway = HD // 2
    frequencies = np.float32(rope_base) ** (-(np.arange(halfway, dtype=np.float32) * np.float32(2.0) / np.float32(HD)))
    angles = np.arange(SEQ, dtype=np.float32)[:, None] * frequencies[None, :].astype(np.float32)
    cosine, sine = np.cos(angles), np.sin(angles)
    return (
        np.concatenate([cosine, cosine], axis=1).astype(np.float32),
        np.concatenate([-sine, sine], axis=1).astype(np.float32),
    )


def contract_last(left, right):
    return lax.dot_general(left, right, (((1,), (1,)), ((), ())), preferred_element_type=F32)


def attend_kernel(sub, tensor_count, per_dp, heads, len_ref, id_ref, cos_ref, sin_ref, q_ref, k_ref, v_ref, out_ref):
    length = len_ref[pl.program_id(0)]
    ids = id_ref[...]
    if sub:
        ids = ((ids % per_dp) // sub) * (q_ref.shape[1] // tensor_count) + (ids // per_dp) * sub + ids % sub
    vocab = q_ref.shape[1]
    one_hot = jnp.where(
        ids == lax.broadcasted_iota(jnp.int32, (SEQ, vocab), 1), 1.0, 0.0
    ).astype(BF16)
    cosine, sine = cos_ref[...], sin_ref[...]

    def rotate(x):
        return (x * cosine + pltpu.roll(x, HD // 2, 1) * sine).astype(BF16)

    keys = rotate(jnp.dot(one_hot, k_ref[0], preferred_element_type=F32))
    values = jnp.dot(one_hot, v_ref[0], preferred_element_type=F32).astype(BF16)
    row = lax.broadcasted_iota(jnp.int32, (SEQ, SEQ), 0)
    column = lax.broadcasted_iota(jnp.int32, (SEQ, SEQ), 1)
    allowed = (column <= row) & (column < length)
    for block in range(heads * HD // WIDE):
        picked = jnp.dot(one_hot, q_ref[block], preferred_element_type=F32)
        for inner in range(WIDE // HD):
            queries = rotate(picked[:, inner * HD : (inner + 1) * HD])
            scores = contract_last(queries, keys) * (1.0 / math.sqrt(HD))
            scores = jnp.where(allowed, scores, -1e30)
            exponent = jnp.exp(scores - jnp.max(scores, axis=1, keepdims=True))
            total = jnp.sum(exponent, axis=1, keepdims=True)
            probs = (exponent * (1.0 / total)).astype(BF16)
            start = block * WIDE + inner * HD
            out_ref[:, start : start + HD] = jnp.dot(
                probs, values, preferred_element_type=F32
            ).astype(BF16)


def table_kernel(
    T, DP, emb, gain, wq, kvw, out,
    rows_in, nrm, xt, wbuf, psend, pown, precv, zsend, zown, zrecv,
    w_sem, kv_send, kv_recv, e_send, e_recv, a_send, a_recv, x_send, x_recv,
    p_send, p_recv, z_send, z_recv, g_send, g_recv, f_send, f_recv,
):
    t = lax.axis_index("tensor")
    d = lax.axis_index("dp")
    Z = DP // 2
    z, core = d // 2, d % 2
    partner = d + 1 - 2 * core
    sub = nrm.shape[1]
    width = nrm.shape[2]
    per = rows_in.shape[2] // width
    nq = wq.shape[0]
    C = wbuf.shape[0]
    seg = zown.shape[1]

    def remote(src, dst, send, recv, **where):
        return pltpu.make_async_remote_copy(
            src_ref=src, dst_ref=dst, send_sem=send, recv_sem=recv, device_id=where, device_id_type=MESH
        )

    load_q = pltpu.make_async_copy(wq, wbuf.at[pl.ds(0, nq)], w_sem)
    load_q.start()

    barrier = pltpu.get_barrier_semaphore()
    for o in range(1, T):
        pl.semaphore_signal(barrier, inc=1, device_id={"tensor": (t + o) % T}, device_id_type=MESH)
    for o in range(1, DP):
        pl.semaphore_signal(barrier, inc=1, device_id={"dp": (d + o) % DP}, device_id_type=MESH)
    pl.semaphore_wait(barrier, T - 1 + DP - 1)

    def e_copy(o):
        p = (t + o) % T
        return remote(
            emb.at[pl.ds(pl.multiple_of(p * sub, sub), sub)], rows_in.at[t], e_send.at[o - 1], e_recv.at[o - 1], tensor=p
        )

    for o in range(1, T):
        e_copy(o).start()

    need = kvw.shape[0] * T // 2 // T
    half = T // 2
    spread = kvw.shape[0] // need
    slot = t // half

    def kv_part(p):
        return kvw.at[pl.ds(pl.multiple_of((p % spread) * need, need), need)]

    def kv_copy(p):
        return remote(kv_part(p), wbuf.at[nq + slot], kv_send.at[p % spread], kv_recv.at[slot], tensor=p)

    for o in range(1, T):
        p = (t + o) % T

        @pl.when(p // spread == t % half)
        def _():
            kv_copy(p).start()

    @pl.when(t // spread == t % half)
    def _():
        pltpu.make_async_copy(kv_part(t), wbuf.at[nq + slot], kv_recv.at[slot]).start()

    rows_in[t] = emb[pl.ds(pl.multiple_of(t * sub, sub), sub), :]
    for o in range(1, T):
        e_copy(o).wait_recv()
    total = jnp.zeros((sub, 1), F32)
    for k in range(T):
        x = rows_in[k].astype(F32)
        total = total + jnp.sum(x * x, axis=1, keepdims=True)
    scale = lax.rsqrt(total / (DP * width) + epsilon)
    for k in range(DP):
        x = rows_in[k // per, :, (k % per) * width : (k % per + 1) * width].astype(F32)
        nrm[k] = (x * scale * gain[:, k * width : (k + 1) * width]).astype(BF16)

    def a_copy(o):
        p = (d + o) % DP
        return remote(nrm.at[p], xt.at[t, d], a_send.at[o - 1], a_recv.at[o - 1], dp=p)

    for o in range(1, DP):
        a_copy(o).start()
    xt[t, d] = nrm[d]

    def x_copy(o, piece):
        source = (d + DP - piece) % DP
        return remote(
            nrm.at[d] if piece == 0 else xt.at[t, source], xt.at[t, source], x_send.at[o - 1, piece], x_recv.at[o - 1, piece],
            tensor=(t + o) % T,
        )

    for piece in range(DP):
        if piece:
            a_copy(piece).wait_recv()
        for o in range(1, T):
            x_copy(o, piece).start()

    load_q.wait()
    for k in range(2):
        pltpu.make_async_copy(wbuf.at[nq + k], wbuf.at[nq + k], kv_recv.at[k]).wait()
    for piece in range(DP):
        for o in range(1, T):
            x_copy(o, piece).wait_recv()

    def half_rows(which):
        return xt[pl.ds(which * half, half)].reshape(Z * seg, width)

    def p_copy(c):
        return remote(psend.at[c], precv.at[c], p_send.at[c], p_recv.at[c], dp=partner)

    def z_copy(o, c):
        there = (z + o) % Z
        return remote(
            zsend.at[c, there], zrecv.at[o - 1, c], z_send.at[o - 1, c], z_recv.at[o - 1, c], dp=there * 2 + core
        )

    def matmuls(c, _):
        psend[c] = contract_last(half_rows(1 - core), wbuf[c])
        p_copy(c).start()
        pown[c] = contract_last(half_rows(core), wbuf[c])
        return 0

    def pair_sums(c, _):
        p_copy(c).wait_recv()
        both = (pown[c] + precv[c]).reshape(Z, seg, WIDE)
        zsend[c] = both.astype(BF16)
        for o in range(1, Z):
            z_copy(o, c).start()
        pown[c] = both.reshape(Z * seg, WIDE)
        zown[c] = pown[c, pl.ds(pl.multiple_of(z * seg, seg), seg), :]
        return 0

    def matmul_then_pair(c, _):
        matmuls(c, 0)
        return pair_sums(c - 1, 0)

    matmuls(0, 0)
    lax.fori_loop(1, C, matmul_then_pair, 0)
    pair_sums(C - 1, 0)

    def chunk(c, which_core, which_z):
        return out.at[c, pl.ds(pl.multiple_of((which_core * Z + which_z) * seg, seg), seg)]

    def g_copy(o, c):
        mine = chunk(c, core, z)
        return remote(mine, mine, g_send.at[o - 1, c], g_recv.at[o - 1, c], dp=((z + o) % Z) * 2 + core)

    def f_copy(o, c):
        piece = chunk(c, core, (z + Z - o) % Z)
        return remote(piece, piece, f_send.at[o, c], f_recv.at[o, c], dp=partner)

    def finish(c, _):
        acc = zown[c]
        for o in range(1, Z):
            z_copy(o, c).wait_recv()
            acc = acc + zrecv[o - 1, c].astype(F32)
        out[c, pl.ds(pl.multiple_of((core * Z + z) * seg, seg), seg), :] = acc.astype(BF16)
        for o in range(1, Z):
            g_copy(o, c).start()
        f_copy(0, c).start()
        return 0

    lax.fori_loop(0, C, finish, 0)

    def forward(c, _):
        for o in range(1, Z):
            g_copy(o, c).wait_recv()
            f_copy(o, c).start()
        return 0

    lax.fori_loop(0, C, forward, 0)

    def drain(c, _):
        for o in range(Z):
            f_copy(o, c).wait()
        p_copy(c).wait_send()
        for o in range(1, Z):
            z_copy(o, c).wait_send()
            g_copy(o, c).wait_send()
        return 0

    lax.fori_loop(0, C, drain, 0)
    for o in range(1, T):
        e_copy(o).wait_send()
        p = (t + o) % T

        @pl.when(p // spread == t % half)
        def _():
            kv_copy(p).wait_send()

        for piece in range(DP):
            x_copy(o, piece).wait_send()
    for o in range(1, DP):
        a_copy(o).wait_send()


def table_by_kernel(embed_table, norm_gain, query_weight, kv_weight):
    T, DP = lax.axis_size("tensor"), lax.axis_size("dp")
    vocab = embed_table.shape[0] * DP
    width = query_weight.shape[1]
    sub = embed_table.shape[0] // T
    nq = query_weight.shape[0] // WIDE
    C = nq + 2
    Z = DP // 2
    seg = vocab // DP
    dma = pltpu.SemaphoreType.DMA
    return pl.pallas_call(
        functools.partial(table_kernel, T, DP),
        out_shape=jax.ShapeDtypeStruct((C, vocab, WIDE), BF16),
        in_specs=[
            pl.BlockSpec(memory_space=pltpu.VMEM),
            pl.BlockSpec(memory_space=pltpu.VMEM),
            pl.BlockSpec(memory_space=pl.ANY),
            pl.BlockSpec(memory_space=pl.ANY),
        ],
        out_specs=pl.BlockSpec(memory_space=pltpu.VMEM),
        scratch_shapes=[
            pltpu.VMEM((T, sub, embed_table.shape[1]), BF16),
            pltpu.VMEM((DP, sub, width), BF16),
            pltpu.VMEM((T, DP, sub, width), BF16),
            pltpu.VMEM((C, WIDE, width), BF16),
            pltpu.VMEM((C, Z * seg, WIDE), F32),
            pltpu.VMEM((C, Z * seg, WIDE), F32),
            pltpu.VMEM((C, Z * seg, WIDE), F32),
            pltpu.VMEM((C, Z, seg, WIDE), BF16),
            pltpu.VMEM((C, seg, WIDE), F32),
            pltpu.VMEM((Z - 1, C, seg, WIDE), BF16),
            dma(()), dma((2,)), dma((2,)),
            dma((T - 1,)), dma((T - 1,)), dma((DP - 1,)), dma((DP - 1,)),
            dma((T - 1, DP)), dma((T - 1, DP)),
            dma((C,)), dma((C,)), dma((Z - 1, C)), dma((Z - 1, C)),
            dma((Z - 1, C)), dma((Z - 1, C)), dma((Z, C)), dma((Z, C)),
        ],
        compiler_params=pltpu.CompilerParams(
            collective_id=0, has_side_effects=True, vmem_limit_bytes=48 * 1024 * 1024
        ),
        name="vocab_table",
    )(embed_table, norm_gain[None, :], query_weight.reshape(nq, WIDE, width), kv_weight)


def table_by_collectives(embed_table, norm_gain, query_weight, kv_weight, first_kv, kv_count):
    rows = lax.all_gather(embed_table, "tensor", axis=1, tiled=True).astype(F32)
    mean_square = jnp.mean(rows * rows, axis=1, keepdims=True)
    normed_rows = (rows * lax.rsqrt(mean_square + epsilon) * norm_gain[None, :]).astype(BF16)
    normed = lax.all_to_all(normed_rows, "dp", split_axis=1, concat_axis=0, tiled=True)
    kv_grid = lax.all_gather(kv_weight, "tensor", axis=0, tiled=True).reshape(2, KV_HEADS, HD, -1)
    kv_rows = lax.dynamic_slice_in_dim(kv_grid, first_kv, kv_count, 1).reshape(2, kv_count * HD, -1)
    kv_rows = jnp.pad(kv_rows, ((0, 0), (0, -kv_count * HD % WIDE), (0, 0))).reshape(-1, kv_rows.shape[2])
    weights = jnp.concatenate([query_weight, kv_rows], axis=0)
    summed = lax.psum_scatter(contract_last(normed, weights), "dp", scatter_dimension=0, tiled=True)
    table = lax.all_gather(summed.astype(BF16), "dp", axis=0, tiled=True)
    return table.reshape(table.shape[0], -1, WIDE).transpose(1, 0, 2)


def on_device(token_ids, seq_lengths, embed_table, norm_gain, query_weight, kv_weight):
    tok_rows = token_ids.shape[0]
    tensor_count, dp_count = lax.axis_size("tensor"), lax.axis_size("dp")
    heads_here = query_weight.shape[0] // HD
    group_size = HEADS // KV_HEADS
    kv_count = max(1, heads_here // group_size)
    per_dp = embed_table.shape[0]
    vocab = per_dp * dp_count
    sub = per_dp // tensor_count
    if sub % 16 == 0 and kv_count * HD == WIDE and tensor_count % 2 == 0 and dp_count % 2 == 0:
        table = table_by_kernel(embed_table, norm_gain, query_weight, kv_weight)
    else:
        sub = 0
        first_kv = lax.axis_index("tensor") * heads_here // group_size
        table = table_by_collectives(embed_table, norm_gain, query_weight, kv_weight, first_kv, kv_count)
    heads = min(4, heads_here)
    blocks = heads * HD // WIDE
    nq = heads_here * HD // WIDE
    nkv = kv_count * HD // WIDE if kv_count * HD >= WIDE else 1
    per_group = heads_here // kv_count
    lanes = WIDE // HD
    cosine, sine = rope_tables()
    whole = pl.BlockSpec((SEQ, HD), lambda s, j: (0, 0))

    def kv_spec(which):
        def index(s, j):
            group = j * heads // per_group
            return (nq + which * nkv + group // lanes, 0, group % lanes)

        return pl.BlockSpec((1, vocab, HD), index)

    return pl.pallas_call(
        functools.partial(attend_kernel, sub, tensor_count, per_dp, heads),
        grid=(tok_rows // SEQ, heads_here // heads),
        out_shape=jax.ShapeDtypeStruct((tok_rows, heads_here * HD), BF16),
        in_specs=[
            pl.BlockSpec(memory_space=pltpu.SMEM),
            pl.BlockSpec((SEQ, 1), lambda s, j: (s, 0)),
            whole,
            whole,
            pl.BlockSpec((blocks, vocab, WIDE), lambda s, j: (j, 0, 0)),
            kv_spec(0),
            kv_spec(1),
        ],
        out_specs=pl.BlockSpec((SEQ, heads * HD), lambda s, j: (s, j)),
        name="attend",
    )(seq_lengths, token_ids[:, None], cosine, sine, table, table, table)


def solution(mesh):
    placed = (P("dp"), P("dp"), P("dp", "tensor"), P(), P("tensor", "dp"), P("tensor", "dp"))
    return jax.shard_map(
        on_device, mesh=mesh, in_specs=placed, out_specs=P("dp", "tensor"), check_vma=False
    )
```

```python
import math

import functools

import jax
import jax.numpy as jnp
import numpy as np
from jax import lax
from jax.experimental import pallas as pl
from jax.experimental.pallas import tpu as pltpu
from jax.sharding import PartitionSpec as P

HD = 128
HEADS = 64
KV_HEADS = 8
SEQ = 256


epsilon = 1e-05
rope_base = 500000.0


MESH = pl.DeviceIdType.MESH
F32 = jnp.float32
BF16 = jnp.bfloat16
WIDE = 256


def rope_tables():
    halfway = HD // 2
    frequencies = np.float32(rope_base) ** (-(np.arange(halfway, dtype=np.float32) * np.float32(2.0) / np.float32(HD)))
    angles = np.arange(SEQ, dtype=np.float32)[:, None] * frequencies[None, :].astype(np.float32)
    cosine, sine = np.cos(angles), np.sin(angles)
    return (
        np.concatenate([cosine, cosine], axis=1).astype(np.float32),
        np.concatenate([-sine, sine], axis=1).astype(np.float32),
    )


def contract_last(left, right):
    return lax.dot_general(left, right, (((1,), (1,)), ((), ())), preferred_element_type=F32)


def attend_kernel(sub, tensor_count, per_dp, heads, nkv, len_ref, id_ref, cos_ref, sin_ref, table, out_ref, picker):
    length = len_ref[pl.program_id(0)]
    vocab = table.shape[1]

    @pl.when(pl.program_id(1) == 0)
    def _():
        ids = id_ref[0]
        if sub:
            ids = ((ids % per_dp) // sub) * (vocab // tensor_count) + (ids // per_dp) * sub + ids % sub
        hits = jnp.where(ids == lax.broadcasted_iota(jnp.int32, (vocab, SEQ), 0), 1.0, 0.0)
        picker[...] = hits.T.astype(BF16)

    one_hot = picker[...]
    group = pl.program_id(1)
    lane = pl.ds(pl.multiple_of(group % (WIDE // HD) * HD, HD), HD)
    part = group // (WIDE // HD)
    cosine, sine = cos_ref[...], sin_ref[...]

    def rotate(x):
        return (x * cosine + pltpu.roll(x, HD // 2, 1) * sine).astype(BF16)

    keys = rotate(jnp.dot(one_hot, table[part, :, lane], preferred_element_type=F32))
    values = jnp.dot(one_hot, table[nkv + part, :, lane], preferred_element_type=F32).astype(BF16)
    row = lax.broadcasted_iota(jnp.int32, (SEQ, SEQ), 0)
    column = lax.broadcasted_iota(jnp.int32, (SEQ, SEQ), 1)
    allowed = (column <= row) & (column < length)
    for block in range(heads * HD // WIDE):
        picked = jnp.dot(one_hot, table[2 * nkv + group * (heads * HD // WIDE) + block], preferred_element_type=F32)
        for inner in range(WIDE // HD):
            queries = rotate(picked[:, inner * HD : (inner + 1) * HD])
            scores = contract_last(queries, keys) * (1.0 / math.sqrt(HD))
            scores = jnp.where(allowed, scores, -1e30)
            exponent = jnp.exp(scores - jnp.max(scores, axis=1, keepdims=True))
            total = jnp.sum(exponent, axis=1, keepdims=True)
            probs = (exponent * (1.0 / total)).astype(BF16)
            start = block * WIDE + inner * HD
            out_ref[:, start : start + HD] = jnp.dot(
                probs, values, preferred_element_type=F32
            ).astype(BF16)


def table_kernel(
    T, DP, emb_in, gain_in, wq, kvw, out,
    emb, gain, rows_in, nrm, xt, wbuf, psend, pown, precv, zsend, right, left, kvout,
    w_sem, e_send, e_recv, a_send, a_recv, x_send, x_recv,
    p_send, p_recv, r_send, r_recv, l_send, l_recv, k_send, k_recv, g_send, g_recv, f_send, f_recv,
):
    t = lax.axis_index("tensor")
    d = lax.axis_index("dp")
    Z = DP // 2
    z, core = d // 2, d % 2
    partner = d + 1 - 2 * core
    sub = nrm.shape[1]
    width = nrm.shape[2]
    per = rows_in.shape[2] // width
    nq = wq.shape[0]
    nkv = kvw.shape[0]
    C = wbuf.shape[0]
    seg = kvout.shape[1]

    def remote(src, dst, send, recv, **where):
        return pltpu.make_async_remote_copy(
            src_ref=src, dst_ref=dst, send_sem=send, recv_sem=recv, device_id=where, device_id_type=MESH
        )

    loads = (
        pltpu.make_async_copy(emb_in, emb, w_sem.at[0]),
        pltpu.make_async_copy(gain_in, gain, w_sem.at[1]),
        pltpu.make_async_copy(kvw, wbuf.at[pl.ds(0, nkv)], w_sem.at[2]),
        pltpu.make_async_copy(wq, wbuf.at[pl.ds(nkv, nq)], w_sem.at[3]),
    )
    for load in loads:
        load.start()

    barrier = pltpu.get_barrier_semaphore()
    for o in range(1, T):
        pl.semaphore_signal(barrier, inc=1, device_id={"tensor": (t + o) % T}, device_id_type=MESH)
    for o in range(1, DP):
        pl.semaphore_signal(barrier, inc=1, device_id={"dp": (d + o) % DP}, device_id_type=MESH)
    loads[0].wait()
    loads[1].wait()
    pl.semaphore_wait(barrier, T - 1 + DP - 1)

    def e_copy(o):
        p = (t + o) % T
        return remote(
            emb.at[pl.ds(pl.multiple_of(p * sub, sub), sub)], rows_in.at[t], e_send.at[o - 1], e_recv.at[o - 1], tensor=p
        )

    for o in range(1, T):
        e_copy(o).start()
    rows_in[t] = emb[pl.ds(pl.multiple_of(t * sub, sub), sub), :]
    for o in range(1, T):
        e_copy(o).wait_recv()
    total = jnp.zeros((sub, 1), F32)
    for k in range(T):
        x = rows_in[k].astype(F32)
        total = total + jnp.sum(x * x, axis=1, keepdims=True)
    scale = lax.rsqrt(total / (DP * width) + epsilon)
    for k in range(DP):
        x = rows_in[k // per, :, (k % per) * width : (k % per + 1) * width].astype(F32)
        nrm[k] = (x * scale * gain[:, k * width : (k + 1) * width]).astype(BF16)

    def a_copy(o):
        p = (d + o) % DP
        return remote(nrm.at[p], xt.at[t, d], a_send.at[o - 1], a_recv.at[o - 1], dp=p)

    for o in range(1, DP):
        a_copy(o).start()
    xt[t, d] = nrm[d]

    def x_copy(o, piece):
        source = (d + DP - piece) % DP
        return remote(
            nrm.at[d] if piece == 0 else xt.at[t, source], xt.at[t, source], x_send.at[o - 1, piece], x_recv.at[o - 1, piece],
            tensor=(t + o) % T,
        )

    for piece in range(DP):
        if piece:
            a_copy(piece).wait_recv()
        for o in range(1, T):
            x_copy(o, piece).start()

    loads[2].wait()
    loads[3].wait()
    for piece in range(DP):
        for o in range(1, T):
            x_copy(o, piece).wait_recv()

    half = T // 2

    def half_rows(which):
        return xt[pl.ds(which * half, half)].reshape(Z * seg, width)

    def p_copy(c):
        return remote(psend.at[c], precv.at[c], p_send.at[c], p_recv.at[c], dp=partner)

    def r_copy(c, k):
        return remote(zsend.at[c, k], right.at[c, k], r_send.at[c, k], r_recv.at[c, k], dp=(z + 1) % Z * 2 + core)

    def l_copy(c, k):
        return remote(zsend.at[c, k], left.at[c, k], l_send.at[c, k], l_recv.at[c, k], dp=(z + Z - 1) % Z * 2 + core)

    def matmuls(c):
        psend[c] = contract_last(half_rows(1 - core), wbuf[c])
        p_copy(c).start()
        pown[c] = contract_last(half_rows(core), wbuf[c]).reshape(Z, seg, WIDE)

    def pair_sums(c):
        p_copy(c).wait_recv()
        pown[c] = pown[c] + precv[c].reshape(Z, seg, WIDE)

        @pl.when(z == 0)
        def _():
            for k in range(Z - 1, 0, -1):
                zsend[c, k] = pown[c, k].astype(BF16)
                r_copy(c, k).start()

        @pl.when(z == Z - 1)
        def _():
            for k in range(Z - 1):
                zsend[c, k] = pown[c, k].astype(BF16)
                l_copy(c, k).start()

    def relay(place):
        def run(c):
            @pl.when(z == place)
            def _():
                for k in range(Z - 1, place, -1):
                    r_copy(c, k).wait_recv()
                    zsend[c, k] = (pown[c, k] + right[c, k].astype(F32)).astype(BF16)
                    r_copy(c, k).start()

            @pl.when(z == Z - 1 - place)
            def _():
                for k in range(Z - 1 - place):
                    l_copy(c, k).wait_recv()
                    zsend[c, k] = (pown[c, k] + left[c, k].astype(F32)).astype(BF16)
                    l_copy(c, k).start()

        return run

    def chunk(c, which_core, which_z):
        return out.at[c, pl.ds(pl.multiple_of((which_core * Z + which_z) * seg, seg), seg)]

    slot = t // half

    def k_copy(c):
        return remote(
            kvout.at[c], chunk(slot, core, z), k_send.at[c], k_recv.at[slot], tensor=(t % half) * nkv + c
        )

    def kv_here(c):
        return (t % half) * nkv + c == t

    def finish(c):
        @pl.when(z > 0)
        def _():
            r_copy(c, z).wait_recv()
            pown[c, z] = pown[c, z] + right[c, z].astype(F32)

        @pl.when(z < Z - 1)
        def _():
            l_copy(c, z).wait_recv()
            pown[c, z] = pown[c, z] + left[c, z].astype(F32)

        result = pown[c, z].astype(BF16)
        rows = pl.ds(pl.multiple_of((core * Z + z) * seg, seg), seg)

        @pl.when(c >= nkv)
        def _():
            out[c, rows, :] = result
            g_start(c, z)

        @pl.when(c < nkv)
        def _():
            kvout[c] = result

            @pl.when(kv_here(c))
            def _():
                out[slot, rows, :] = result

            @pl.when(jnp.logical_not(kv_here(c)))
            def _():
                k_copy(c).start()

    def g_copy(c, k, there):
        piece = chunk(c, core, k)
        way = 0 if there == 1 else 1
        return remote(
            piece, piece, g_send.at[way, c, k], g_recv.at[c, k], dp=(z + Z + there) % Z * 2 + core
        )

    def f_copy(c, k):
        piece = chunk(c, core, k)
        return remote(piece, piece, f_send.at[c, k], f_recv.at[c, k], dp=partner)

    def g_start(c, k):
        @pl.when((k <= z) & (z < Z - 1))
        def _():
            g_copy(c, k, 1).start()

        @pl.when((k >= z) & (z > 0))
        def _():
            g_copy(c, k, -1).start()

        f_copy(c, k).start()

    def kv_gather(c):
        @pl.when(c < nkv)
        def _():
            source = c * half + t // nkv

            @pl.when(source != t)
            def _():
                pltpu.make_async_copy(kvout.at[0], chunk(c, core, z), k_recv.at[c]).wait()

            g_start(c, z)

    def g_relay(distance):
        def run(c):
            @pl.when(z >= distance)
            def _():
                g_copy(c, z - distance, 1).wait_recv()
                g_start(c, z - distance)

            @pl.when(z + distance < Z)
            def _():
                g_copy(c, z + distance, -1).wait_recv()
                g_start(c, z + distance)

        return run

    stages = [(0, matmuls), (1, pair_sums)]
    lag = 1
    for place in range(1, Z - 1):
        lag += 1
        stages.append((lag, relay(place)))
    lag += 1
    stages.append((lag, finish))
    lag += 1
    stages.append((lag, kv_gather))
    for distance in range(1, Z):
        stages.append((lag + distance - 1, g_relay(distance)))

    def step(i, _):
        for behind, stage in stages:
            @pl.when((i >= behind) & (i < C + behind))
            def _():
                stage(i - behind)

        return 0

    lax.fori_loop(0, C + stages[-1][0], step, 0)

    def drain(c, _):
        p_copy(c).wait_send()
        for k in range(Z):
            f_copy(c, k).wait()

            @pl.when(k > z)
            def _():
                r_copy(c, k).wait_send()

            @pl.when(k < z)
            def _():
                l_copy(c, k).wait_send()

            @pl.when((k <= z) & (z < Z - 1))
            def _():
                g_copy(c, k, 1).wait_send()

            @pl.when((k >= z) & (z > 0))
            def _():
                g_copy(c, k, -1).wait_send()

        return 0

    lax.fori_loop(0, C, drain, 0)
    for c in range(nkv):
        @pl.when(jnp.logical_not(kv_here(c)))
        def _():
            k_copy(c).wait_send()

    for o in range(1, T):
        e_copy(o).wait_send()
        for piece in range(DP):
            x_copy(o, piece).wait_send()
    for o in range(1, DP):
        a_copy(o).wait_send()


def table_by_kernel(embed_table, norm_gain, query_weight, kv_weight):
    T, DP = lax.axis_size("tensor"), lax.axis_size("dp")
    vocab = embed_table.shape[0] * DP
    width = query_weight.shape[1]
    sub = embed_table.shape[0] // T
    nq = query_weight.shape[0] // WIDE
    nkv = kv_weight.shape[0] // WIDE
    C = nq + nkv
    Z = DP // 2
    seg = vocab // DP
    dma = pltpu.SemaphoreType.DMA
    return pl.pallas_call(
        functools.partial(table_kernel, T, DP),
        out_shape=jax.ShapeDtypeStruct((C, vocab, WIDE), BF16),
        in_specs=[pl.BlockSpec(memory_space=pl.ANY)] * 4,
        out_specs=pl.BlockSpec(memory_space=pltpu.VMEM),
        scratch_shapes=[
            pltpu.VMEM(embed_table.shape, BF16),
            pltpu.VMEM((1, norm_gain.shape[0]), F32),
            pltpu.VMEM((T, sub, embed_table.shape[1]), BF16),
            pltpu.VMEM((DP, sub, width), BF16),
            pltpu.VMEM((T, DP, sub, width), BF16),
            pltpu.VMEM((C, WIDE, width), BF16),
            pltpu.VMEM((C, Z * seg, WIDE), F32),
            pltpu.VMEM((C, Z, seg, WIDE), F32),
            pltpu.VMEM((C, Z * seg, WIDE), F32),
            pltpu.VMEM((C, Z, seg, WIDE), BF16),
            pltpu.VMEM((C, Z, seg, WIDE), BF16),
            pltpu.VMEM((C, Z, seg, WIDE), BF16),
            pltpu.VMEM((nkv, seg, WIDE), BF16),
            dma((4,)), dma((T - 1,)), dma((T - 1,)), dma((DP - 1,)), dma((DP - 1,)),
            dma((T - 1, DP)), dma((T - 1, DP)),
            dma((C,)), dma((C,)), dma((C, Z)), dma((C, Z)), dma((C, Z)), dma((C, Z)),
            dma((nkv,)), dma((nkv,)), dma((2, C, Z)), dma((C, Z)), dma((C, Z)), dma((C, Z)),
        ],
        compiler_params=pltpu.CompilerParams(
            collective_id=0, has_side_effects=True, vmem_limit_bytes=56 * 1024 * 1024
        ),
        name="vocab_table",
    )(
        embed_table, norm_gain[None, :], query_weight.reshape(nq, WIDE, width), kv_weight.reshape(nkv, WIDE, width)
    )


def table_by_collectives(embed_table, norm_gain, query_weight, kv_weight, first_kv, kv_count):
    rows = lax.all_gather(embed_table, "tensor", axis=1, tiled=True).astype(F32)
    mean_square = jnp.mean(rows * rows, axis=1, keepdims=True)
    normed_rows = (rows * lax.rsqrt(mean_square + epsilon) * norm_gain[None, :]).astype(BF16)
    normed = lax.all_to_all(normed_rows, "dp", split_axis=1, concat_axis=0, tiled=True)
    kv_grid = lax.all_gather(kv_weight, "tensor", axis=0, tiled=True).reshape(2, KV_HEADS, HD, -1)
    kv_rows = lax.dynamic_slice_in_dim(kv_grid, first_kv, kv_count, 1).reshape(2, kv_count * HD, -1)
    kv_rows = jnp.pad(kv_rows, ((0, 0), (0, -kv_count * HD % WIDE), (0, 0))).reshape(-1, kv_rows.shape[2])
    weights = jnp.concatenate([kv_rows, query_weight], axis=0)
    summed = lax.psum_scatter(contract_last(normed, weights), "dp", scatter_dimension=0, tiled=True)
    table = lax.all_gather(summed.astype(BF16), "dp", axis=0, tiled=True)
    return table.reshape(table.shape[0], -1, WIDE).transpose(1, 0, 2)


def on_device(token_ids, seq_lengths, embed_table, norm_gain, query_weight, kv_weight):
    tok_rows = token_ids.shape[0]
    tensor_count, dp_count = lax.axis_size("tensor"), lax.axis_size("dp")
    heads_here = query_weight.shape[0] // HD
    group_size = HEADS // KV_HEADS
    kv_count = max(1, heads_here // group_size)
    per_dp = embed_table.shape[0]
    vocab = per_dp * dp_count
    sub = per_dp // tensor_count
    if sub % 16 == 0 and kv_count * HD == WIDE and tensor_count == 4 and dp_count % 2 == 0:
        table = table_by_kernel(embed_table, norm_gain, query_weight, kv_weight)
    else:
        sub = 0
        first_kv = lax.axis_index("tensor") * heads_here // group_size
        table = table_by_collectives(embed_table, norm_gain, query_weight, kv_weight, first_kv, kv_count)
    per_group = heads_here // kv_count
    cosine, sine = rope_tables()
    whole = pl.BlockSpec((SEQ, HD), lambda s, j: (0, 0))
    return pl.pallas_call(
        functools.partial(attend_kernel, sub, tensor_count, per_dp, per_group, max(1, kv_count * HD // WIDE)),
        grid=(tok_rows // SEQ, kv_count),
        out_shape=jax.ShapeDtypeStruct((tok_rows, heads_here * HD), BF16),
        in_specs=[
            pl.BlockSpec(memory_space=pltpu.SMEM),
            pl.BlockSpec((1, 1, SEQ), lambda s, j: (s, 0, 0)),
            whole,
            whole,
            pl.BlockSpec(memory_space=pltpu.VMEM),
        ],
        out_specs=pl.BlockSpec((SEQ, per_group * HD), lambda s, j: (s, j)),
        scratch_shapes=[pltpu.VMEM((SEQ, vocab), BF16)],
        name="attend",
    )(seq_lengths, token_ids.reshape(-1, 1, SEQ), cosine, sine, table)


def solution(mesh):
    placed = (P("dp"), P("dp"), P("dp", "tensor"), P(), P("tensor", "dp"), P("tensor", "dp"))
    return jax.shard_map(
        on_device, mesh=mesh, in_specs=placed, out_specs=P("dp", "tensor"), check_vma=False
    )
```

```python
import math

import functools

import jax
import jax.numpy as jnp
import numpy as np
from jax import lax
from jax.experimental import pallas as pl
from jax.experimental.pallas import tpu as pltpu
from jax.sharding import PartitionSpec as P

HD = 128
HEADS = 64
KV_HEADS = 8
SEQ = 256


epsilon = 1e-05
rope_base = 500000.0


MESH = pl.DeviceIdType.MESH
F32 = jnp.float32
BF16 = jnp.bfloat16
WIDE = 256


def rope_tables():
    halfway = HD // 2
    frequencies = np.float32(rope_base) ** (-(np.arange(halfway, dtype=np.float32) * np.float32(2.0) / np.float32(HD)))
    angles = np.arange(SEQ, dtype=np.float32)[:, None] * frequencies[None, :].astype(np.float32)
    cosine, sine = np.cos(angles), np.sin(angles)
    return (
        np.concatenate([cosine, cosine], axis=1).astype(np.float32),
        np.concatenate([-sine, sine], axis=1).astype(np.float32),
    )


def contract_last(left, right):
    return lax.dot_general(left, right, (((1,), (1,)), ((), ())), preferred_element_type=F32)


def attend_kernel(sub, tensor_count, per_dp, heads, nkv, len_ref, id_ref, cos_ref, sin_ref, table, out_ref, picker):
    length = len_ref[pl.program_id(0)]
    vocab = table.shape[1]

    @pl.when(pl.program_id(1) == 0)
    def _():
        ids = id_ref[0]
        if sub:
            ids = ((ids % per_dp) // sub) * (vocab // tensor_count) + (ids // per_dp) * sub + ids % sub
        hits = jnp.where(ids == lax.broadcasted_iota(jnp.int32, (vocab, SEQ), 0), 1.0, 0.0)
        picker[...] = hits.T.astype(BF16)

    one_hot = picker[...]
    group = pl.program_id(1)
    lane = pl.ds(pl.multiple_of(group % (WIDE // HD) * HD, HD), HD)
    part = group // (WIDE // HD)
    cosine, sine = cos_ref[...], sin_ref[...]

    def rotate(x):
        return (x * cosine + pltpu.roll(x, HD // 2, 1) * sine).astype(BF16)

    keys = rotate(jnp.dot(one_hot, table[part, :, lane], preferred_element_type=F32))
    values = jnp.dot(one_hot, table[nkv + part, :, lane], preferred_element_type=F32).astype(BF16)
    parts = []
    for first, last in ((0, SEQ // 2), (SEQ // 2, SEQ)):
        row = lax.broadcasted_iota(jnp.int32, (last - first, last), 0) + first
        column = lax.broadcasted_iota(jnp.int32, (last - first, last), 1)
        parts.append((first, last, (column <= row) & (column < length)))
    for block in range(heads * HD // WIDE):
        picked = jnp.dot(
            one_hot, table[2 * nkv + group * (heads * HD // WIDE) + block], preferred_element_type=F32
        )
        for inner in range(WIDE // HD):
            queries = rotate(picked[:, inner * HD : (inner + 1) * HD])
            start = block * WIDE + inner * HD
            for first, last, allowed in parts:
                scores = contract_last(queries[first:last], keys[:last]) * (1.0 / math.sqrt(HD))
                scores = jnp.where(allowed, scores, -1e30)
                exponent = jnp.exp(scores - jnp.max(scores, axis=1, keepdims=True))
                total = jnp.sum(exponent, axis=1, keepdims=True)
                probs = (exponent * (1.0 / total)).astype(BF16)
                out_ref[first:last, start : start + HD] = jnp.dot(
                    probs, values[:last], preferred_element_type=F32
                ).astype(BF16)


def table_kernel(
    T, DP, per_dp, emb_in, gain_in, wq, kvw, len_ref, id_ref, cos_ref, sin_ref, att,
    out, picker, keys, values,
    emb, gain, rows_in, nrm, xt, wbuf, psend, pown, precv, zsend, right, left, kvout,
    w_sem, e_send, e_recv, a_send, a_recv, x_send, x_recv,
    p_send, p_recv, r_send, r_recv, l_send, l_recv, k_send, k_recv, g_send, g_recv, f_send, f_recv,
):
    t = lax.axis_index("tensor")
    d = lax.axis_index("dp")
    Z = DP // 2
    z, core = d // 2, d % 2
    partner = d + 1 - 2 * core
    sub = nrm.shape[1]
    width = nrm.shape[2]
    per = rows_in.shape[2] // width
    nq = wq.shape[0]
    nkv = kvw.shape[0]
    C = wbuf.shape[0]
    seg = kvout.shape[1]

    def remote(src, dst, send, recv, **where):
        return pltpu.make_async_remote_copy(
            src_ref=src, dst_ref=dst, send_sem=send, recv_sem=recv, device_id=where, device_id_type=MESH
        )

    loads = (
        pltpu.make_async_copy(emb_in, emb, w_sem.at[0]),
        pltpu.make_async_copy(gain_in, gain, w_sem.at[1]),
        pltpu.make_async_copy(kvw, wbuf.at[pl.ds(0, nkv)], w_sem.at[2]),
        pltpu.make_async_copy(wq, wbuf.at[pl.ds(nkv, nq)], w_sem.at[3]),
    )
    for load in loads:
        load.start()
    vocab = out.shape[1]
    seqs = id_ref.shape[0]
    for q in range(seqs):
        ids = id_ref[q]
        ids = ((ids % per_dp) // sub) * (vocab // T) + (ids // per_dp) * sub + ids % sub
        hits = jnp.where(ids == lax.broadcasted_iota(jnp.int32, (vocab, SEQ), 0), 1.0, 0.0)
        picker[q] = hits.T.astype(BF16)

    barrier = pltpu.get_barrier_semaphore()
    for o in range(1, T):
        pl.semaphore_signal(barrier, inc=1, device_id={"tensor": (t + o) % T}, device_id_type=MESH)
    for o in range(1, DP):
        pl.semaphore_signal(barrier, inc=1, device_id={"dp": (d + o) % DP}, device_id_type=MESH)
    loads[0].wait()
    loads[1].wait()
    pl.semaphore_wait(barrier, T - 1 + DP - 1)

    def e_copy(o):
        p = (t + o) % T
        return remote(
            emb.at[pl.ds(pl.multiple_of(p * sub, sub), sub)], rows_in.at[t], e_send.at[o - 1], e_recv.at[o - 1], tensor=p
        )

    for o in range(1, T):
        e_copy(o).start()
    rows_in[t] = emb[pl.ds(pl.multiple_of(t * sub, sub), sub), :]
    for o in range(1, T):
        e_copy(o).wait_recv()
    total = jnp.zeros((sub, 1), F32)
    for k in range(T):
        x = rows_in[k].astype(F32)
        total = total + jnp.sum(x * x, axis=1, keepdims=True)
    scale = lax.rsqrt(total / (DP * width) + epsilon)
    for k in range(DP):
        x = rows_in[k // per, :, (k % per) * width : (k % per + 1) * width].astype(F32)
        nrm[k] = (x * scale * gain[:, k * width : (k + 1) * width]).astype(BF16)

    def a_copy(o):
        p = (d + o) % DP
        return remote(nrm.at[p], xt.at[t, d], a_send.at[o - 1], a_recv.at[o - 1], dp=p)

    for o in range(1, DP):
        a_copy(o).start()
    xt[t, d] = nrm[d]

    def x_copy(o, piece):
        source = (d + DP - piece) % DP
        return remote(
            nrm.at[d] if piece == 0 else xt.at[t, source], xt.at[t, source], x_send.at[o - 1, piece], x_recv.at[o - 1, piece],
            tensor=(t + o) % T,
        )

    for piece in range(DP):
        if piece:
            a_copy(piece).wait_recv()
        for o in range(1, T):
            x_copy(o, piece).start()

    loads[2].wait()
    loads[3].wait()
    for piece in range(DP):
        for o in range(1, T):
            x_copy(o, piece).wait_recv()

    half = T // 2

    def half_rows(which):
        return xt[pl.ds(which * half, half)].reshape(Z * seg, width)

    def p_copy(c):
        return remote(psend.at[c], precv.at[c], p_send.at[c], p_recv.at[c], dp=partner)

    def r_copy(c, k):
        return remote(zsend.at[c, k], right.at[c, k], r_send.at[c, k], r_recv.at[c, k], dp=(z + 1) % Z * 2 + core)

    def l_copy(c, k):
        return remote(zsend.at[c, k], left.at[c, k], l_send.at[c, k], l_recv.at[c, k], dp=(z + Z - 1) % Z * 2 + core)

    def matmuls(c):
        psend[c] = contract_last(half_rows(1 - core), wbuf[c])
        p_copy(c).start()
        pown[c] = contract_last(half_rows(core), wbuf[c]).reshape(Z, seg, WIDE)

    def pair_sums(c):
        p_copy(c).wait_recv()
        pown[c] = pown[c] + precv[c].reshape(Z, seg, WIDE)

        @pl.when(z == 0)
        def _():
            for k in range(Z - 1, 0, -1):
                zsend[c, k] = pown[c, k].astype(BF16)
                r_copy(c, k).start()

        @pl.when(z == Z - 1)
        def _():
            for k in range(Z - 1):
                zsend[c, k] = pown[c, k].astype(BF16)
                l_copy(c, k).start()

    def relay(place):
        def run(c):
            @pl.when(z == place)
            def _():
                for k in range(Z - 1, place, -1):
                    r_copy(c, k).wait_recv()
                    zsend[c, k] = (pown[c, k] + right[c, k].astype(F32)).astype(BF16)
                    r_copy(c, k).start()

            @pl.when(z == Z - 1 - place)
            def _():
                for k in range(Z - 1 - place):
                    l_copy(c, k).wait_recv()
                    zsend[c, k] = (pown[c, k] + left[c, k].astype(F32)).astype(BF16)
                    l_copy(c, k).start()

        return run

    def chunk(c, which_core, which_z):
        return out.at[c, pl.ds(pl.multiple_of((which_core * Z + which_z) * seg, seg), seg)]

    slot = t // half

    def k_copy(c):
        return remote(
            kvout.at[c], chunk(slot, core, z), k_send.at[c], k_recv.at[slot], tensor=(t % half) * nkv + c
        )

    def kv_here(c):
        return (t % half) * nkv + c == t

    def finish(c):
        @pl.when(z > 0)
        def _():
            r_copy(c, z).wait_recv()
            pown[c, z] = pown[c, z] + right[c, z].astype(F32)

        @pl.when(z < Z - 1)
        def _():
            l_copy(c, z).wait_recv()
            pown[c, z] = pown[c, z] + left[c, z].astype(F32)

        result = pown[c, z].astype(BF16)
        rows = pl.ds(pl.multiple_of((core * Z + z) * seg, seg), seg)

        @pl.when(c >= nkv)
        def _():
            out[c, rows, :] = result
            g_start(c, z)

        @pl.when(c < nkv)
        def _():
            kvout[c] = result

            @pl.when(kv_here(c))
            def _():
                out[slot, rows, :] = result

            @pl.when(jnp.logical_not(kv_here(c)))
            def _():
                k_copy(c).start()

    def g_copy(c, k, there):
        piece = chunk(c, core, k)
        way = 0 if there == 1 else 1
        return remote(
            piece, piece, g_send.at[way, c, k], g_recv.at[c, k], dp=(z + Z + there) % Z * 2 + core
        )

    def f_copy(c, k):
        piece = chunk(c, core, k)
        return remote(piece, piece, f_send.at[c, k], f_recv.at[c, k], dp=partner)

    def g_start(c, k):
        @pl.when((k <= z) & (z < Z - 1))
        def _():
            g_copy(c, k, 1).start()

        @pl.when((k >= z) & (z > 0))
        def _():
            g_copy(c, k, -1).start()

        f_copy(c, k).start()

    def kv_gather(c):
        @pl.when(c < nkv)
        def _():
            source = c * half + t // nkv

            @pl.when(source != t)
            def _():
                pltpu.make_async_copy(kvout.at[0], chunk(c, core, z), k_recv.at[c]).wait()

            g_start(c, z)

    def g_relay(distance):
        def run(c):
            @pl.when(z >= distance)
            def _():
                g_copy(c, z - distance, 1).wait_recv()
                g_start(c, z - distance)

            @pl.when(z + distance < Z)
            def _():
                g_copy(c, z + distance, -1).wait_recv()
                g_start(c, z + distance)

        return run

    stages = [(0, matmuls), (1, pair_sums)]
    lag = 1
    for place in range(1, Z - 1):
        lag += 1
        stages.append((lag, relay(place)))
    lag += 1
    stages.append((lag, finish))
    lag += 1
    stages.append((lag, kv_gather))
    for distance in range(1, Z):
        stages.append((lag + distance - 1, g_relay(distance)))

    def rotate(x):
        return (x * cos_ref[...] + pltpu.roll(x, HD // 2, 1) * sin_ref[...]).astype(BF16)

    lanes = WIDE // HD

    def attend(c):
        for k in range(Z):
            f_copy(c, k).wait_recv()

        @pl.when(c == 0)
        def _():
            for q in range(seqs):
                picked = jnp.dot(picker[q], out[0], preferred_element_type=F32)
                for g in range(lanes):
                    keys[g, q] = rotate(picked[:, g * HD : (g + 1) * HD])

        @pl.when(c == 1)
        def _():
            for q in range(seqs):
                picked = jnp.dot(picker[q], out[1], preferred_element_type=F32).astype(BF16)
                for g in range(lanes):
                    values[g, q] = picked[:, g * HD : (g + 1) * HD]

        @pl.when(c >= nkv)
        def _():
            block = c - nkv
            group = block // (nq // lanes)
            for q in range(seqs):
                picked = jnp.dot(picker[q], out[c], preferred_element_type=F32)
                for inner in range(lanes):
                    queries = rotate(picked[:, inner * HD : (inner + 1) * HD])
                    lane = pl.ds(pl.multiple_of(block * WIDE + inner * HD, HD), HD)
                    for first, last in ((0, SEQ // 2), (SEQ // 2, SEQ)):
                        row = lax.broadcasted_iota(jnp.int32, (last - first, last), 0) + first
                        column = lax.broadcasted_iota(jnp.int32, (last - first, last), 1)
                        allowed = (column <= row) & (column < len_ref[q])
                        scores = contract_last(queries[first:last], keys[group, q, :last]) * (1.0 / math.sqrt(HD))
                        scores = jnp.where(allowed, scores, -1e30)
                        exponent = jnp.exp(scores - jnp.max(scores, axis=1, keepdims=True))
                        total = jnp.sum(exponent, axis=1, keepdims=True)
                        probs = (exponent * (1.0 / total)).astype(BF16)
                        att[q * SEQ + first : q * SEQ + last, lane] = jnp.dot(
                            probs, values[group, q, :last], preferred_element_type=F32
                        ).astype(BF16)

    stages.append((stages[-1][0] + 1, attend))

    def step(i, _):
        for behind, stage in stages:
            @pl.when((i >= behind) & (i < C + behind))
            def _():
                stage(i - behind)

        return 0

    lax.fori_loop(0, C + stages[-1][0], step, 0)

    def drain(c, _):
        p_copy(c).wait_send()
        for k in range(Z):
            f_copy(c, k).wait_send()

            @pl.when(k > z)
            def _():
                r_copy(c, k).wait_send()

            @pl.when(k < z)
            def _():
                l_copy(c, k).wait_send()

            @pl.when((k <= z) & (z < Z - 1))
            def _():
                g_copy(c, k, 1).wait_send()

            @pl.when((k >= z) & (z > 0))
            def _():
                g_copy(c, k, -1).wait_send()

        return 0

    lax.fori_loop(0, C, drain, 0)
    for c in range(nkv):
        @pl.when(jnp.logical_not(kv_here(c)))
        def _():
            k_copy(c).wait_send()

    for o in range(1, T):
        e_copy(o).wait_send()
        for piece in range(DP):
            x_copy(o, piece).wait_send()
    for o in range(1, DP):
        a_copy(o).wait_send()


def attend_by_kernel(token_ids, seq_lengths, embed_table, norm_gain, query_weight, kv_weight):
    T, DP = lax.axis_size("tensor"), lax.axis_size("dp")
    vocab = embed_table.shape[0] * DP
    width = query_weight.shape[1]
    sub = embed_table.shape[0] // T
    nq = query_weight.shape[0] // WIDE
    nkv = kv_weight.shape[0] // WIDE
    C = nq + nkv
    Z = DP // 2
    seg = vocab // DP
    seqs = token_ids.shape[0] // SEQ
    dma = pltpu.SemaphoreType.DMA
    return pl.pallas_call(
        functools.partial(table_kernel, T, DP, embed_table.shape[0]),
        out_shape=jax.ShapeDtypeStruct((token_ids.shape[0], nq * WIDE), BF16),
        in_specs=[pl.BlockSpec(memory_space=pl.ANY)] * 4
        + [pl.BlockSpec(memory_space=pltpu.SMEM)]
        + [pl.BlockSpec(memory_space=pltpu.VMEM)] * 3,
        out_specs=pl.BlockSpec(memory_space=pltpu.VMEM),
        scratch_shapes=[
            pltpu.VMEM((C, vocab, WIDE), BF16),
            pltpu.VMEM((seqs, SEQ, vocab), BF16),
            pltpu.VMEM((WIDE // HD, seqs, SEQ, HD), BF16),
            pltpu.VMEM((WIDE // HD, seqs, SEQ, HD), BF16),
            pltpu.VMEM(embed_table.shape, BF16),
            pltpu.VMEM((1, norm_gain.shape[0]), F32),
            pltpu.VMEM((T, sub, embed_table.shape[1]), BF16),
            pltpu.VMEM((DP, sub, width), BF16),
            pltpu.VMEM((T, DP, sub, width), BF16),
            pltpu.VMEM((C, WIDE, width), BF16),
            pltpu.VMEM((C, Z * seg, WIDE), F32),
            pltpu.VMEM((C, Z, seg, WIDE), F32),
            pltpu.VMEM((C, Z * seg, WIDE), F32),
            pltpu.VMEM((C, Z, seg, WIDE), BF16),
            pltpu.VMEM((C, Z, seg, WIDE), BF16),
            pltpu.VMEM((C, Z, seg, WIDE), BF16),
            pltpu.VMEM((nkv, seg, WIDE), BF16),
            dma((4,)), dma((T - 1,)), dma((T - 1,)), dma((DP - 1,)), dma((DP - 1,)),
            dma((T - 1, DP)), dma((T - 1, DP)),
            dma((C,)), dma((C,)), dma((C, Z)), dma((C, Z)), dma((C, Z)), dma((C, Z)),
            dma((nkv,)), dma((nkv,)), dma((2, C, Z)), dma((C, Z)), dma((C, Z)), dma((C, Z)),
        ],
        compiler_params=pltpu.CompilerParams(
            collective_id=0, has_side_effects=True, vmem_limit_bytes=56 * 1024 * 1024
        ),
        name="table_attend",
    )(
        embed_table, norm_gain[None, :], query_weight.reshape(nq, WIDE, width), kv_weight.reshape(nkv, WIDE, width),
        seq_lengths, token_ids.reshape(-1, 1, SEQ), *rope_tables()
    )


def table_by_collectives(embed_table, norm_gain, query_weight, kv_weight, first_kv, kv_count):
    rows = lax.all_gather(embed_table, "tensor", axis=1, tiled=True).astype(F32)
    mean_square = jnp.mean(rows * rows, axis=1, keepdims=True)
    normed_rows = (rows * lax.rsqrt(mean_square + epsilon) * norm_gain[None, :]).astype(BF16)
    normed = lax.all_to_all(normed_rows, "dp", split_axis=1, concat_axis=0, tiled=True)
    kv_grid = lax.all_gather(kv_weight, "tensor", axis=0, tiled=True).reshape(2, KV_HEADS, HD, -1)
    kv_rows = lax.dynamic_slice_in_dim(kv_grid, first_kv, kv_count, 1).reshape(2, kv_count * HD, -1)
    kv_rows = jnp.pad(kv_rows, ((0, 0), (0, -kv_count * HD % WIDE), (0, 0))).reshape(-1, kv_rows.shape[2])
    weights = jnp.concatenate([kv_rows, query_weight], axis=0)
    summed = lax.psum_scatter(contract_last(normed, weights), "dp", scatter_dimension=0, tiled=True)
    table = lax.all_gather(summed.astype(BF16), "dp", axis=0, tiled=True)
    return table.reshape(table.shape[0], -1, WIDE).transpose(1, 0, 2)


def on_device(token_ids, seq_lengths, embed_table, norm_gain, query_weight, kv_weight):
    tok_rows = token_ids.shape[0]
    tensor_count, dp_count = lax.axis_size("tensor"), lax.axis_size("dp")
    heads_here = query_weight.shape[0] // HD
    group_size = HEADS // KV_HEADS
    kv_count = max(1, heads_here // group_size)
    per_dp = embed_table.shape[0]
    vocab = per_dp * dp_count
    sub = per_dp // tensor_count
    if sub % 16 == 0 and kv_count * HD == WIDE and tensor_count == 4 and dp_count % 2 == 0:
        return attend_by_kernel(token_ids, seq_lengths, embed_table, norm_gain, query_weight, kv_weight)
    sub = 0
    first_kv = lax.axis_index("tensor") * heads_here // group_size
    table = table_by_collectives(embed_table, norm_gain, query_weight, kv_weight, first_kv, kv_count)
    per_group = heads_here // kv_count
    cosine, sine = rope_tables()
    whole = pl.BlockSpec((SEQ, HD), lambda s, j: (0, 0))
    return pl.pallas_call(
        functools.partial(attend_kernel, sub, tensor_count, per_dp, per_group, max(1, kv_count * HD // WIDE)),
        grid=(tok_rows // SEQ, kv_count),
        out_shape=jax.ShapeDtypeStruct((tok_rows, heads_here * HD), BF16),
        in_specs=[
            pl.BlockSpec(memory_space=pltpu.SMEM),
            pl.BlockSpec((1, 1, SEQ), lambda s, j: (s, 0, 0)),
            whole,
            whole,
            pl.BlockSpec(memory_space=pltpu.VMEM),
        ],
        out_specs=pl.BlockSpec((SEQ, per_group * HD), lambda s, j: (s, j)),
        scratch_shapes=[pltpu.VMEM((SEQ, vocab), BF16)],
        name="attend",
    )(seq_lengths, token_ids.reshape(-1, 1, SEQ), cosine, sine, table)


def solution(mesh):
    placed = (P("dp"), P("dp"), P("dp", "tensor"), P(), P("tensor", "dp"), P("tensor", "dp"))
    return jax.shard_map(
        on_device, mesh=mesh, in_specs=placed, out_specs=P("dp", "tensor"), check_vma=False
    )
```
